1024 devices in a mesh: dp: 64 (over z, core), cols: 16 (over y, x).
Axes of the slice: x: 4, y: 4, z: 32, core: 2. Of those that a mesh axis runs over, the one named last changes fastest.
Arguments:
- kv_latent: bfloat16 [8192, 512], P('dp', 'cols'), may hold values from -6 to 6
- kv_grad_out: bfloat16 [8192, 16384], P('dp'), may hold values from -8 to 8
- kv_weight: float32 [512, 16384], P('cols', 'dp'), may hold values from -6 to 6
- logit_max: float32 [64, 64], P('dp'), may hold values from 1 to 600, as said below
Outputs:
- kv_new: float32 [512, 16384], P('cols', 'dp')
The draws below stay inside these ranges and needn't reach their ends.
Inputs may be any that keep to these rules, and one draw needn't show every extreme that they name: `logit_max`: each entry is a largest attention logit of one head over one index of dp's tokens.
All inputs are finite; a program needn't handle non-finite values.
Results may differ from the reference program's by a relative error of at most 0.0003.
Values sent between devices are 32-bit elements; how exact they have to be, the bound alone decides.
No kernel may reach another device: no remote copies, remote signals or barrier semaphores. Data moves between devices by JAX's collectives and lax.ppermute only.
A program may use at most 32 MiB of HBM per device.

```python
import math
import jax
import jax.numpy as jnp
from jax import lax

KR = 512
NOPE = 128
VD = 128
TOK_DEV = 128
ITERS = 2
KD = 256
HEADS = 64
TOKENS = 8192


def draw_logit_max(key, part):
    ranks = TOKENS // TOK_DEV
    key_base = jax.random.fold_in(key, 11)
    key_jitter = jax.random.fold_in(key, 23)
    base = jnp.exp(jax.random.uniform(key_base, (HEADS,), jnp.float32, jnp.log(40.0), jnp.log(400.0)))
    position = jnp.arange(ranks, dtype=jnp.float32) / max(ranks - 1, 1)
    rise = jnp.exp((position - 1.0) * jnp.log(3.0))
    jitter = jax.random.uniform(key_jitter, (ranks, HEADS), jnp.float32, 0.85, 1.0)
    return (base[None, :] * rise[:, None] * jitter).astype(jnp.float32)


def with_spikes(drawn, key, source, target, parts, factor):
    def block_of(dim):
        return (jnp.arange(drawn.shape[dim]) // (drawn.shape[dim] // parts)).reshape((-1,) + (1,) * (drawn.ndim - 1 - dim))

    one_side = jax.random.permutation(key, parts)[block_of(target)]
    second = (block_of(target) + parts // 2) % parts
    return jnp.where((block_of(source) == one_side) | (block_of(source) == second), factor * drawn, drawn)


def block_levels(key, dims, pieces, low, largest):
    factor_of = 1.0
    for dim, blocks in pieces:
        draws = jax.random.uniform(jax.random.fold_in(jax.random.fold_in(key, 6), dim), (blocks,), jnp.float32, low / len(pieces), largest / len(pieces))
        factor_of = factor_of * jnp.repeat(jnp.exp(draws), dims[dim] // blocks).reshape((-1,) + (1,) * (len(dims) - 1 - dim))
    return factor_of


def gaussian(rng, shape, deviation, limit, shards=(), kind=jnp.bfloat16):
    gain = block_levels(rng, shape, shards, -0.22, 0.18) if shards else 1.0
    result = jax.random.normal(rng, shape, jnp.float32) * deviation * gain
    return jnp.minimum(jnp.maximum(result, -limit), limit).astype(kind)


def gaussian_with(key, dims, scale, limit, pieces, heavy, kind=jnp.bfloat16):
    result = scale * jax.random.normal(key, dims, jnp.float32)
    if pieces:
        result = result * block_levels(key, dims, pieces, -0.22, 0.18)
    return jnp.clip(with_spikes(result, jax.random.fold_in(key, 3), *heavy), -limit, limit).astype(kind)


def setup_inputs(seed: int = 0) -> dict:
    splits = jax.random.split(jax.random.key(seed), 5)
    kv_latent = gaussian(splits[0], (TOKENS, KR), 1.0, 6.0, ((0, 64), (1, 16)))
    kv_grad_out = gaussian_with(splits[1], (TOKENS, HEADS * KD), 1.0, 8.0, ((0, 64),), (0, 1, 64, 4.0))
    kv_weight = gaussian(splits[2], (KR, HEADS * KD), 1.0, 6.0, ((0, 16), (1, 64)), jnp.float32)
    logit_max = draw_logit_max(jax.random.fold_in(splits[4], 71), 0)
    return {"kv_latent": kv_latent, "kv_grad_out": kv_grad_out, "kv_weight": kv_weight, "logit_max": logit_max}


coef_first = 3.4445
coef_second = -4.775
coef_third = 2.0315
tau_logit = 100.0
learn_rate = 0.5
decay_rate = 0.1
highest = lax.Precision.HIGHEST

def orthogonalize(block):
    norm_value = jnp.sqrt(jnp.sum(block * block))
    current = block / (norm_value + 1e-07)
    for step in range(ITERS):
        gram = jnp.dot(current, current.T, precision=highest)
        square = jnp.dot(gram, gram, precision=highest)
        poly = coef_second * gram + coef_third * square
        current = coef_first * current + jnp.dot(poly, current, precision=highest)
    return current

def reference(kv_latent, kv_grad_out, kv_weight, logit_max):
    peak = lax.optimization_barrier(jnp.max(logit_max, axis=0))
    ratio = jnp.minimum(1.0, tau_logit / peak)
    root = jnp.sqrt(ratio)
    kv_factor = jnp.concatenate([jnp.broadcast_to(root[:, None], (HEADS, NOPE)), jnp.ones((HEADS, VD), jnp.float32)], axis=1)
    grads = jnp.dot(kv_grad_out.T, kv_latent, preferred_element_type=jnp.float32)
    blocks = grads.reshape(HEADS, KD, KR)
    ortho = lax.map(orthogonalize, blocks)
    columns = jnp.transpose(ortho, (2, 0, 1)).reshape(KR, HEADS * KD)
    scale = 0.2 * math.sqrt(max(KR, KD))
    stepped = kv_weight - learn_rate * (scale * columns + decay_rate * kv_weight)
    return stepped * kv_factor.reshape(1, HEADS * KD)
```

```python
import math

import jax
import jax.numpy as jnp
from jax import lax
from jax.experimental import pallas as pl
from jax.experimental.pallas import tpu as pltpu
from jax.sharding import PartitionSpec as P

KR = 512
NOPE = 128
KD = 256
HALF = 128
CORES = 2
NEAR = 4

coef_first = 3.4445
coef_second = -4.775
coef_third = 2.0315
tau_logit = 100.0
learn_rate = 0.5
decay_rate = 0.1
highest = lax.Precision.HIGHEST


def partial_kernel(parity_ref, latent_ref, grad_ref, logit_ref, out_ref, *, far, feats):
    step = pl.program_id(0)
    rows = 2 * feats
    for near in range(NEAR):
        start = pl.multiple_of((near * CORES + parity_ref[0]) * KD, KD)
        prod = jnp.dot(latent_ref[...], grad_ref[:, pl.ds(start, KD)], preferred_element_type=jnp.float32)
        for half in range(2):
            out_ref[near, pl.ds(step * rows + half * feats, feats), :] = prod[:, half * HALF : (half + 1) * HALF]

    @pl.when(step == 0)
    def _():
        heads = far * NEAR
        row = lax.broadcasted_iota(jnp.int32, (heads, heads * CORES), 0)
        lane = lax.broadcasted_iota(jnp.int32, (heads, heads * CORES), 1)
        owner = (row % far) * (NEAR * CORES) + (row // far) * CORES + parity_ref[0]
        spread = jnp.sum(jnp.where(lane == owner, logit_ref[...], 0.0), axis=1, keepdims=True)
        out_ref[:, far * rows :, :] = jnp.broadcast_to(spread, (heads, HALF)).reshape(NEAR, far, HALF)


def partial_sums(latent, grad, logit, parity, far):
    tokens, width = grad.shape
    feats = latent.shape[0]
    block = width // far
    depth = far * 2 * feats + far
    return pl.pallas_call(
        lambda *refs: partial_kernel(*refs, far=far, feats=feats),
        grid_spec=pltpu.PrefetchScalarGridSpec(
            num_scalar_prefetch=1,
            grid=(far,),
            in_specs=[
                pl.BlockSpec((feats, tokens), lambda i, _: (0, 0)),
                pl.BlockSpec((tokens, block), lambda i, _: (0, i)),
                pl.BlockSpec((1, logit.shape[1]), lambda i, _: (0, 0)),
            ],
            out_specs=pl.BlockSpec((NEAR, depth, HALF), lambda i, _: (0, 0, 0)),
        ),
        out_shape=jax.ShapeDtypeStruct((NEAR, depth, HALF), jnp.float32),
        name="partial_sums",
    )(parity, latent, grad, logit)


def near_kernel(in_ref, out_ref, *, far, rows):
    total = in_ref[0, : far * rows] + in_ref[1, : far * rows] + (in_ref[2, : far * rows] + in_ref[3, : far * rows])
    out_ref[:, :rows, :] = total.reshape(far, rows, HALF)
    tail = jnp.maximum(
        jnp.maximum(in_ref[0, far * rows :], in_ref[1, far * rows :]),
        jnp.maximum(in_ref[2, far * rows :], in_ref[3, far * rows :]),
    )
    out_ref[:, rows:, :] = jnp.broadcast_to(tail[:, None, :], (far, 8, HALF))


def in_vmem(count):
    return [pl.BlockSpec(memory_space=pltpu.VMEM)] * count


def near_sum(parts, far, rows):
    return pl.pallas_call(
        lambda *refs: near_kernel(*refs, far=far, rows=rows),
        in_specs=in_vmem(1),
        out_specs=in_vmem(1)[0],
        out_shape=jax.ShapeDtypeStruct((far, rows + 8, HALF), jnp.float32),
        name="near_sum",
    )(parts)


def far_kernel(in_ref, block_ref, peak_ref, *, rows):
    block_ref[...] = jnp.broadcast_to(jnp.sum(in_ref[:, :rows, :], axis=0), block_ref.shape)
    peak_ref[...] = jnp.max(in_ref[:, rows:, :], axis=0)


def far_sum(parts, rows, copies):
    return pl.pallas_call(
        lambda *refs: far_kernel(*refs, rows=rows),
        in_specs=in_vmem(1),
        out_specs=tuple(in_vmem(2)),
        out_shape=(
            jax.ShapeDtypeStruct((copies, rows, HALF), jnp.float32),
            jax.ShapeDtypeStruct((8, HALF), jnp.float32),
        ),
        name="far_sum",
    )(parts)


def final_kernel(all_ref, own_ref, peak_ref, weight_ref, out_ref, *, feats):
    def mul(left, right):
        return jnp.dot(left, right, precision=highest, preferred_element_type=jnp.float32)

    count = all_ref.shape[0]
    whole = jnp.concatenate(
        [
            all_ref[:, :feats, :].reshape(count * feats, HALF),
            all_ref[:, feats:, :].reshape(count * feats, HALF),
        ],
        axis=1,
    )
    gram = lax.dot_general(
        whole, whole, (((0,), (0,)), ((), ())), precision=highest, preferred_element_type=jnp.float32
    )
    total = jnp.sum(whole * whole)
    row = lax.broadcasted_iota(jnp.int32, (KD, KD), 0)
    col = lax.broadcasted_iota(jnp.int32, (KD, KD), 1)
    eye = jnp.where(row == col, coef_first, 0.0)
    factor = 1.0 / (jnp.sqrt(jnp.broadcast_to(total, (1, KD))) + 1e-07)
    first = gram * (factor * factor)
    poly_first = eye + coef_second * first + coef_third * mul(first, first)
    second = mul(mul(poly_first, first), poly_first)
    poly_second = eye + coef_second * second + coef_third * mul(second, second)
    own = jnp.concatenate([own_ref[0, :feats, :], own_ref[0, feats:, :]], axis=1) * factor
    ortho = mul(mul(own, poly_first), poly_second)
    scale = 0.2 * math.sqrt(max(KR, KD))
    weight = weight_ref[...]
    stepped = weight - learn_rate * (scale * ortho + decay_rate * weight)
    root = jnp.sqrt(jnp.minimum(1.0, tau_logit / peak_ref[:1, :]))
    clip = jnp.concatenate([root, jnp.ones((1, KD - NOPE), jnp.float32)], axis=1)
    out_ref[...] = stepped * clip


def finish(blocks, own, peak, weight):
    return pl.pallas_call(
        lambda *refs: final_kernel(*refs, feats=weight.shape[0]),
        in_specs=in_vmem(4),
        out_specs=in_vmem(1)[0],
        out_shape=jax.ShapeDtypeStruct(weight.shape, jnp.float32),
        name="finish",
    )(blocks, own, peak, weight)


def stage_groups(size):
    chips = size // CORES
    near = []
    for core in range(CORES):
        for window in range(chips // NEAR):
            members = [(NEAR * window + core * (NEAR // 2) + k) % chips for k in range(NEAR)]
            near.append([CORES * z + core for z in sorted(members, key=lambda z: z % NEAR)])
    far = [
        [CORES * z + core for z in range(kind, chips, NEAR)] for kind in range(NEAR) for core in range(CORES)
    ]
    return near, far


def body(kv_latent, kv_grad_out, kv_weight, logit_max, size, cols):
    far = size // (NEAR * CORES)
    feats = kv_latent.shape[1]
    rows = 2 * feats
    near, distant = stage_groups(size)

    def exchange(value, groups):
        return lax.all_to_all(value, "dp", 0, 0, axis_index_groups=groups, tiled=True)

    latent = kv_latent.T
    parity = (lax.axis_index("dp") % CORES).reshape(1)
    sent = partial_sums(latent, kv_grad_out, logit_max, 1 - parity, far)
    taken = lax.ppermute(sent, "dp", [(i, i ^ 1) for i in range(size)])
    kept = partial_sums(latent, kv_grad_out, logit_max, parity, far)
    is_sum = lax.broadcasted_iota(jnp.int32, kept.shape, 1) < far * rows
    parts = jnp.where(is_sum, kept + taken, jnp.maximum(kept, taken))
    parts = exchange(parts, near)
    parts = exchange(near_sum(parts, far, rows), distant)
    copies, peak = far_sum(parts, rows, cols)
    blocks = lax.all_to_all(copies, "cols", 0, 0, tiled=True)
    return finish(blocks, copies, peak, kv_weight)


def solution(mesh):
    in_specs = (P("dp", "cols"), P("dp", None), P("cols", "dp"), P("dp", None))
    out_specs = P("cols", "dp")
    size, cols = mesh.shape["dp"], mesh.shape["cols"]
    return jax.shard_map(
        lambda *args: body(*args, size, cols), mesh=mesh, in_specs=in_specs, out_specs=out_specs, check_vma=False
    )
```

```python
import functools
import math

import jax
import jax.numpy as jnp
from jax import lax
from jax.experimental import pallas as pl
from jax.experimental.pallas import tpu as pltpu
from jax.sharding import PartitionSpec as P

KR = 512
NOPE = 128
KD = 256
HALF = 128
CORES = 2
NEAR = 4
GROUPS = 2

coef_first = 3.4445
coef_second = -4.775
coef_third = 2.0315
tau_logit = 100.0
learn_rate = 0.5
decay_rate = 0.1


def in_vmem(value):
    return pltpu.with_memory_space_constraint(value, pltpu.VMEM)


def partial_kernel(parity_ref, latent_ref, grad_ref, logit_ref, out_ref, buffer, sems, *, far, feats):
    rows = 2 * feats
    heads = far * NEAR
    copies = []
    for head in range(heads):
        start = pl.multiple_of((head * CORES + parity_ref[0]) * KD, KD)
        copies.append(
            pltpu.make_async_copy(
                grad_ref.at[:, pl.ds(start, KD)], buffer.at[:, head * KD : (head + 1) * KD], sems.at[head]
            )
        )
    for copy in copies:
        copy.start()

    row = lax.broadcasted_iota(jnp.int32, (heads, heads * CORES), 0)
    lane = lax.broadcasted_iota(jnp.int32, (heads, heads * CORES), 1)
    owner = (row % far) * (NEAR * CORES) + (row // far) * CORES + parity_ref[0]
    spread = jnp.sum(jnp.where(lane == owner, logit_ref[...], 0.0), axis=1, keepdims=True)
    out_ref[:, far * rows :, :] = jnp.broadcast_to(spread, (heads, HALF)).reshape(NEAR, far, HALF)

    batch = heads // GROUPS
    for group in range(GROUPS):
        members = range(group * batch, (group + 1) * batch)
        for head in members:
            copies[head].wait()
        block = buffer[:, group * batch * KD : (group + 1) * batch * KD]
        prod = jnp.dot(latent_ref[...], block, preferred_element_type=jnp.float32)
        for head in members:
            distant, near = head // NEAR, head % NEAR
            for half in range(2):
                low = (head - group * batch) * KD + half * HALF
                first = distant * rows + half * feats
                out_ref[near, first : first + feats, :] = prod[:, low : low + HALF]


def partial_sums(latent, grad, logit, parity, far):
    feats = latent.shape[0]
    tokens, width = grad.shape
    depth = far * 2 * feats + far
    return pl.pallas_call(
        functools.partial(partial_kernel, far=far, feats=feats),
        in_specs=[
            pl.BlockSpec(memory_space=pltpu.SMEM),
            pl.BlockSpec(memory_space=pltpu.VMEM),
            pl.BlockSpec(memory_space=pl.ANY),
            pl.BlockSpec(memory_space=pltpu.VMEM),
        ],
        out_shape=pltpu.VMEM((NEAR, depth, HALF), jnp.float32),
        scratch_shapes=[
            pltpu.VMEM((tokens, width // CORES), jnp.bfloat16),
            pltpu.SemaphoreType.DMA((far * NEAR,)),
        ],
        name="partial_sums",
    )(parity, latent, grad, logit)


def near_kernel(in_ref, out_ref, *, far, rows):
    depth = far * rows
    for distant in range(far):
        low, high = distant * rows, (distant + 1) * rows
        base = distant * (rows + 1)
        out_ref[base : base + rows, :] = (in_ref[0, low:high] + in_ref[1, low:high]) + (
            in_ref[2, low:high] + in_ref[3, low:high]
        )
    tail = jnp.maximum(
        jnp.maximum(in_ref[0, depth:], in_ref[1, depth:]), jnp.maximum(in_ref[2, depth:], in_ref[3, depth:])
    )
    for distant in range(far):
        base = distant * (rows + 1) + rows
        out_ref[base : base + 1, :] = tail[distant : distant + 1]


def near_sum(parts, far, rows):
    return pl.pallas_call(
        functools.partial(near_kernel, far=far, rows=rows),
        out_shape=pltpu.VMEM((far * (rows + 1), HALF), jnp.float32),
        name="near_sum",
    )(in_vmem(parts))


def far_kernel(in_ref, block_ref, peak_ref, *, far, rows):
    sums = [in_ref[k * (rows + 1) : k * (rows + 1) + rows, :] for k in range(far)]
    peaks = [in_ref[k * (rows + 1) + rows : (k + 1) * (rows + 1), :] for k in range(far)]
    block_ref[...] = jnp.broadcast_to(functools.reduce(jnp.add, sums), block_ref.shape)
    peak_ref[...] = jnp.broadcast_to(functools.reduce(jnp.maximum, peaks), peak_ref.shape)


def far_sum(parts, far, rows, copies):
    return pl.pallas_call(
        functools.partial(far_kernel, far=far, rows=rows),
        out_shape=(pltpu.VMEM((copies, rows, HALF), jnp.float32), pltpu.VMEM((8, HALF), jnp.float32)),
        name="far_sum",
    )(in_vmem(parts))


def parted(value):
    high = value.astype(jnp.bfloat16)
    return high, (value - high.astype(jnp.float32)).astype(jnp.bfloat16)


def single(left, right, dims=(((1,), (0,)), ((), ()))):
    return lax.dot_general(left, right, dims, preferred_element_type=jnp.float32)


def product(left, right):
    return single(left[0], right[0]) + (single(left[0], right[1]) + single(left[1], right[0]))


def final_kernel(all_ref, own_ref, peak_ref, weight_ref, out_ref, *, feats):
    count = all_ref.shape[0]
    whole = jnp.concatenate(
        [
            all_ref[:, :feats, :].reshape(count * feats, HALF),
            all_ref[:, feats:, :].reshape(count * feats, HALF),
        ],
        axis=1,
    )
    high, low = parted(whole)
    over_rows = (((0,), (0,)), ((), ()))
    mixed = single(high, low, over_rows)
    gram = single(high, high, over_rows) + (mixed + mixed.T)
    total = jnp.sum(whole * whole)
    factor = 1.0 / (jnp.sqrt(jnp.broadcast_to(total, (1, KD))) + 1e-07)
    row = lax.broadcasted_iota(jnp.int32, (KD, KD), 0)
    col = lax.broadcasted_iota(jnp.int32, (KD, KD), 1)
    first = gram * (factor * factor)
    split_first = parted(first)
    poly = jnp.where(row == col, coef_first, 0.0) + coef_second * first + coef_third * product(split_first, split_first)
    split_poly = parted(poly)
    own = jnp.concatenate([own_ref[0, :feats, :], own_ref[0, feats:, :]], axis=1) * factor
    current = product(parted(own), split_poly)
    second = parted(product(parted(product(split_poly, split_first)), split_poly))
    once = product(parted(current), second)
    twice = product(parted(once), second)
    ortho = coef_first * current + coef_second * once + coef_third * twice
    scale = 0.2 * math.sqrt(max(KR, KD))
    weight = weight_ref[...]
    stepped = weight - learn_rate * (scale * ortho + decay_rate * weight)
    root = jnp.sqrt(jnp.minimum(1.0, tau_logit / peak_ref[:1, :]))
    clip = jnp.concatenate([root, jnp.ones((1, KD - NOPE), jnp.float32)], axis=1)
    out_ref[...] = stepped * clip


def finish(blocks, own, peak, weight):
    return pl.pallas_call(
        functools.partial(final_kernel, feats=weight.shape[0]),
        out_shape=jax.ShapeDtypeStruct(weight.shape, jnp.float32),
        name="finish",
    )(in_vmem(blocks), in_vmem(own), in_vmem(peak), in_vmem(weight))


def stage_groups(size):
    chips = size // CORES
    near = []
    for core in range(CORES):
        for window in range(chips // NEAR):
            members = [(NEAR * window + core * (NEAR // 2) + k) % chips for k in range(NEAR)]
            near.append([CORES * z + core for z in sorted(members, key=lambda z: z % NEAR)])
    far = [
        [CORES * z + core for z in range(kind, chips, NEAR)] for kind in range(NEAR) for core in range(CORES)
    ]
    return near, far


def body(kv_latent, kv_grad_out, kv_weight, logit_max, size, cols):
    far = size // (NEAR * CORES)
    feats = kv_latent.shape[1]
    rows = 2 * feats
    near, distant = stage_groups(size)

    def exchange(value, groups):
        return lax.all_to_all(value, "dp", 0, 0, axis_index_groups=groups, tiled=True)

    latent = kv_latent.T
    parity = (lax.axis_index("dp") % CORES).reshape(1)
    sent = partial_sums(latent, kv_grad_out, logit_max, 1 - parity, far)
    taken = lax.ppermute(sent, "dp", [(i, i ^ 1) for i in range(size)])
    kept = partial_sums(latent, kv_grad_out, logit_max, parity, far)
    is_sum = lax.broadcasted_iota(jnp.int32, kept.shape, 1) < far * rows
    parts = jnp.where(is_sum, kept + taken, jnp.maximum(kept, taken))
    summed = near_sum(exchange(parts, near), far, rows)
    parts = exchange(summed.reshape(far, 1, -1), distant).reshape(summed.shape)
    copies, peak = far_sum(parts, far, rows, cols)
    blocks = lax.all_to_all(copies, "cols", 0, 0, tiled=True)
    return finish(blocks, copies, peak, kv_weight)


def solution(mesh):
    in_specs = (P("dp", "cols"), P("dp", None), P("cols", "dp"), P("dp", None))
    out_specs = P("cols", "dp")
    size, cols = mesh.shape["dp"], mesh.shape["cols"]
    return jax.shard_map(
        lambda *args: body(*args, size, cols), mesh=mesh, in_specs=in_specs, out_specs=out_specs, check_vma=False
    )
```

```python
import functools
import math

import jax
import jax.numpy as jnp
from jax import lax
from jax.experimental import pallas as pl
from jax.experimental.pallas import tpu as pltpu
from jax.sharding import PartitionSpec as P

KR = 512
NOPE = 128
KD = 256
HALF = 128
CORES = 2
NEAR = 4
GROUPS = 2
FAR_ORDER = (3, 2, 1, 0, 7, 6, 5, 4)
NEAR_ORDER = (3, 2, 1, 0)
COL_ORDER = (15, 14, 13, 12, 11, 10, 9, 8, 7, 6, 5, 4, 3, 2, 1, 0)

coef_first = 3.4445
coef_second = -4.775
coef_third = 2.0315
tau_logit = 100.0
learn_rate = 0.5
decay_rate = 0.1


def in_vmem(value):
    return pltpu.with_memory_space_constraint(value, pltpu.VMEM)


def partial_kernel(latent_hbm, grad_ref, logit_hbm, out_ref, latent_ref, logit_ref, buffer, sems, *, far, feats, other):
    rows = 2 * feats
    heads = far * NEAR
    parity = lax.axis_index("dp") % CORES
    if other:
        parity = 1 - parity
    side = [
        pltpu.make_async_copy(logit_hbm, logit_ref, sems.at[heads]),
        pltpu.make_async_copy(latent_hbm, latent_ref, sems.at[heads + 1]),
    ]
    for copy in side:
        copy.start()
    copies = []
    for head in range(heads):
        start = pl.multiple_of((head * CORES + parity) * KD, KD)
        copies.append(
            pltpu.make_async_copy(
                grad_ref.at[:, pl.ds(start, KD)], buffer.at[:, head * KD : (head + 1) * KD], sems.at[head]
            )
        )
    for copy in copies:
        copy.start()

    for copy in side:
        copy.wait()
    row = lax.broadcasted_iota(jnp.int32, (heads, heads * CORES), 0)
    lane = lax.broadcasted_iota(jnp.int32, (heads, heads * CORES), 1)
    slot = row // far
    kind = sum(jnp.where(slot == k, NEAR_ORDER[k], 0) for k in range(NEAR))
    owner = (row % far) * (NEAR * CORES) + kind * CORES + parity
    spread = jnp.sum(jnp.where(lane == owner, logit_ref[...], 0.0), axis=1, keepdims=True)
    out_ref[:, far * rows :, :] = jnp.broadcast_to(spread, (heads, HALF)).reshape(NEAR, far, HALF)

    batch = heads // GROUPS
    for group in range(GROUPS):
        members = range(group * batch, (group + 1) * batch)
        for head in members:
            copies[head].wait()
        block = buffer[:, group * batch * KD : (group + 1) * batch * KD]
        prod = jnp.dot(latent_ref[...], block, preferred_element_type=jnp.float32)
        for head in members:
            distant, near = head // NEAR, head % NEAR
            for half in range(2):
                low = (head - group * batch) * KD + half * HALF
                first = distant * rows + half * feats
                out_ref[NEAR_ORDER.index(near), first : first + feats, :] = prod[:, low : low + HALF]


def partial_sums(latent, grad, logit, far, other):
    feats = latent.shape[0]
    tokens, width = grad.shape
    depth = far * 2 * feats + far
    return pl.pallas_call(
        functools.partial(partial_kernel, far=far, feats=feats, other=other),
        in_specs=[pl.BlockSpec(memory_space=pl.ANY)] * 3,
        out_shape=pltpu.VMEM((NEAR, depth, HALF), jnp.float32),
        scratch_shapes=[
            pltpu.VMEM(latent.shape, latent.dtype),
            pltpu.VMEM(logit.shape, logit.dtype),
            pltpu.VMEM((tokens, width // CORES), grad.dtype),
            pltpu.SemaphoreType.DMA((far * NEAR + 2,)),
        ],
        name="partial_other" if other else "partial_own",
    )(latent, grad, logit)


def near_kernel(in_ref, out_ref, *, far, rows):
    depth = far * rows
    for distant in range(far):
        low, high = distant * rows, (distant + 1) * rows
        base = FAR_ORDER.index(distant) * (rows + 1)
        out_ref[base : base + rows, :] = (in_ref[0, low:high] + in_ref[1, low:high]) + (
            in_ref[2, low:high] + in_ref[3, low:high]
        )
    tail = jnp.maximum(
        jnp.maximum(in_ref[0, depth:], in_ref[1, depth:]), jnp.maximum(in_ref[2, depth:], in_ref[3, depth:])
    )
    for distant in range(far):
        base = FAR_ORDER.index(distant) * (rows + 1) + rows
        out_ref[base : base + 1, :] = tail[distant : distant + 1]


def near_sum(parts, far, rows):
    return pl.pallas_call(
        functools.partial(near_kernel, far=far, rows=rows),
        out_shape=pltpu.VMEM((far * (rows + 1), HALF), jnp.float32),
        name="near_sum",
    )(in_vmem(parts))


def far_kernel(in_ref, block_ref, peak_ref, *, far, rows):
    sums = [in_ref[k * (rows + 1) : k * (rows + 1) + rows, :] for k in range(far)]
    peaks = [in_ref[k * (rows + 1) + rows : (k + 1) * (rows + 1), :] for k in range(far)]
    block_ref[...] = jnp.broadcast_to(functools.reduce(jnp.add, sums), block_ref.shape)
    peak_ref[...] = jnp.broadcast_to(functools.reduce(jnp.maximum, peaks), peak_ref.shape)


def far_sum(parts, far, rows, copies):
    return pl.pallas_call(
        functools.partial(far_kernel, far=far, rows=rows),
        out_shape=(pltpu.VMEM((copies, rows, HALF), jnp.float32), pltpu.VMEM((8, HALF), jnp.float32)),
        name="far_sum",
    )(in_vmem(parts))


def parted(value):
    high = value.astype(jnp.bfloat16)
    return high, (value - high.astype(jnp.float32)).astype(jnp.bfloat16)


def single(left, right, dims=(((1,), (0,)), ((), ()))):
    return lax.dot_general(left, right, dims, preferred_element_type=jnp.float32)


def product(left, right):
    return single(left[0], right[0]) + (single(left[0], right[1]) + single(left[1], right[0]))


def final_kernel(all_ref, own_ref, peak_ref, weight_ref, out_ref, *, feats):
    count = all_ref.shape[0]
    whole = jnp.concatenate(
        [
            all_ref[:, :feats, :].reshape(count * feats, HALF),
            all_ref[:, feats:, :].reshape(count * feats, HALF),
        ],
        axis=1,
    )
    high, low = parted(whole)
    over_rows = (((0,), (0,)), ((), ()))
    mixed = single(high, low, over_rows)
    gram = single(high, high, over_rows) + (mixed + mixed.T)
    total = jnp.sum(whole * whole)
    factor = 1.0 / (jnp.sqrt(jnp.broadcast_to(total, (1, KD))) + 1e-07)
    row = lax.broadcasted_iota(jnp.int32, (KD, KD), 0)
    col = lax.broadcasted_iota(jnp.int32, (KD, KD), 1)
    first = gram * (factor * factor)
    split_first = parted(first)
    poly = jnp.where(row == col, coef_first, 0.0) + coef_second * first + coef_third * product(split_first, split_first)
    split_poly = parted(poly)
    own = jnp.concatenate([own_ref[0, :feats, :], own_ref[0, feats:, :]], axis=1) * factor
    current = product(parted(own), split_poly)
    second = parted(product(parted(product(split_poly, split_first)), split_poly))
    once = product(parted(current), second)
    twice = product(parted(once), second)
    ortho = coef_first * current + coef_second * once + coef_third * twice
    scale = 0.2 * math.sqrt(max(KR, KD))
    weight = weight_ref[...]
    stepped = weight - learn_rate * (scale * ortho + decay_rate * weight)
    root = jnp.sqrt(jnp.minimum(1.0, tau_logit / peak_ref[:1, :]))
    clip = jnp.concatenate([root, jnp.ones((1, KD - NOPE), jnp.float32)], axis=1)
    out_ref[...] = stepped * clip


def finish(blocks, own, peak, weight):
    return pl.pallas_call(
        functools.partial(final_kernel, feats=weight.shape[0]),
        out_shape=jax.ShapeDtypeStruct(weight.shape, jnp.float32),
        name="finish",
    )(in_vmem(blocks), in_vmem(own), in_vmem(peak), in_vmem(weight))


def stage_groups(size):
    chips = size // CORES
    near = []
    for core in range(CORES):
        for window in range(chips // NEAR):
            members = [(NEAR * window + core * (NEAR // 2) + k) % chips for k in range(NEAR)]
            near.append([CORES * z + core for z in sorted(members, key=lambda z: NEAR_ORDER.index(z % NEAR))])
    far = [
        [CORES * (kind + NEAR * k) + core for k in FAR_ORDER] for kind in range(NEAR) for core in range(CORES)
    ]
    return near, far


def body(kv_latent, kv_grad_out, kv_weight, logit_max, size, cols):
    far = size // (NEAR * CORES)
    feats = kv_latent.shape[1]
    rows = 2 * feats
    near, distant = stage_groups(size)

    def exchange(value, groups):
        return lax.all_to_all(value, "dp", 0, 0, axis_index_groups=groups, tiled=True)

    latent = kv_latent.T
    sent = partial_sums(latent, kv_grad_out, logit_max, far, True)
    taken = lax.ppermute(sent, "dp", [(i, i ^ 1) for i in range(size)])
    kept = partial_sums(latent, kv_grad_out, logit_max, far, False)
    is_sum = lax.broadcasted_iota(jnp.int32, kept.shape, 1) < far * rows
    parts = jnp.where(is_sum, kept + taken, jnp.maximum(kept, taken))
    summed = near_sum(exchange(parts, near), far, rows)
    parts = exchange(summed.reshape(far, 1, -1), distant).reshape(summed.shape)
    copies, peak = far_sum(parts, far, rows, cols)
    blocks = lax.all_to_all(copies, "cols", 0, 0, axis_index_groups=[list(COL_ORDER)], tiled=True)
    return finish(blocks, copies, peak, kv_weight)


def solution(mesh):
    in_specs = (P("dp", "cols"), P("dp", None), P("cols", "dp"), P("dp", None))
    out_specs = P("cols", "dp")
    size, cols = mesh.shape["dp"], mesh.shape["cols"]
    return jax.shard_map(
        lambda *args: body(*args, size, cols), mesh=mesh, in_specs=in_specs, out_specs=out_specs, check_vma=False
    )
```

```python
import functools
import math

import jax
import jax.numpy as jnp
from jax import lax
from jax.experimental import pallas as pl
from jax.experimental.pallas import tpu as pltpu
from jax.sharding import PartitionSpec as P

KR = 512
NOPE = 128
KD = 256
HALF = 128
CORES = 2
NEAR = 4
GROUPS = 2
FAR_ORDER = (4, 3, 2, 1, 0, 7, 6, 5)
NEAR_ORDER = (1, 0, 3, 2)
COL_ORDER = (15, 14, 13, 12, 11, 10, 9, 8, 7, 6, 5, 4, 3, 2, 1, 0)

coef_first = 3.4445
coef_second = -4.775
coef_third = 2.0315
tau_logit = 100.0
learn_rate = 0.5
decay_rate = 0.1


def in_vmem(value):
    return pltpu.with_memory_space_constraint(value, pltpu.VMEM)


def partial_kernel(latent_hbm, grad_ref, logit_hbm, out_ref, latent_ref, logit_ref, buffer, sems, *, far, feats, other):
    rows = 2 * feats
    heads = far * NEAR
    parity = lax.axis_index("dp") % CORES
    if other:
        parity = 1 - parity
    side = [
        pltpu.make_async_copy(logit_hbm, logit_ref, sems.at[heads]),
        pltpu.make_async_copy(latent_hbm, latent_ref, sems.at[heads + 1]),
    ]
    for copy in side:
        copy.start()
    copies = []
    for head in range(heads):
        start = pl.multiple_of((head * CORES + parity) * KD, KD)
        copies.append(
            pltpu.make_async_copy(
                grad_ref.at[:, pl.ds(start, KD)], buffer.at[:, head * KD : (head + 1) * KD], sems.at[head]
            )
        )
    for copy in copies:
        copy.start()

    for copy in side:
        copy.wait()
    row = lax.broadcasted_iota(jnp.int32, (heads, heads * CORES), 0)
    lane = lax.broadcasted_iota(jnp.int32, (heads, heads * CORES), 1)
    slot = row // far
    kind = sum(jnp.where(slot == k, NEAR_ORDER[k], 0) for k in range(NEAR))
    owner = (row % far) * (NEAR * CORES) + kind * CORES + parity
    spread = jnp.sum(jnp.where(lane == owner, logit_ref[...], 0.0), axis=1, keepdims=True)
    out_ref[:, far * rows :, :] = jnp.broadcast_to(spread, (heads, HALF)).reshape(NEAR, far, HALF)

    batch = heads // GROUPS
    for group in range(GROUPS):
        members = range(group * batch, (group + 1) * batch)
        for head in members:
            copies[head].wait()
        block = buffer[:, group * batch * KD : (group + 1) * batch * KD]
        prod = jnp.dot(latent_ref[...], block, preferred_element_type=jnp.float32)
        for head in members:
            distant, near = head // NEAR, head % NEAR
            for half in range(2):
                low = (head - group * batch) * KD + half * HALF
                first = distant * rows + half * feats
                out_ref[NEAR_ORDER.index(near), first : first + feats, :] = prod[:, low : low + HALF]


def partial_sums(latent, grad, logit, far, other):
    feats = latent.shape[0]
    tokens, width = grad.shape
    depth = far * 2 * feats + far
    return pl.pallas_call(
        functools.partial(partial_kernel, far=far, feats=feats, other=other),
        in_specs=[pl.BlockSpec(memory_space=pl.ANY)] * 3,
        out_shape=pltpu.VMEM((NEAR, depth, HALF), jnp.float32),
        scratch_shapes=[
            pltpu.VMEM(latent.shape, latent.dtype),
            pltpu.VMEM(logit.shape, logit.dtype),
            pltpu.VMEM((tokens, width // CORES), grad.dtype),
            pltpu.SemaphoreType.DMA((far * NEAR + 2,)),
        ],
        name="partial_other" if other else "partial_own",
    )(latent, grad, logit)


def near_kernel(in_ref, out_ref, *, far, rows):
    depth = far * rows
    for distant in range(far):
        low, high = distant * rows, (distant + 1) * rows
        base = FAR_ORDER.index(distant) * (rows + 1)
        out_ref[base : base + rows, :] = (in_ref[0, low:high] + in_ref[1, low:high]) + (
            in_ref[2, low:high] + in_ref[3, low:high]
        )
    tail = jnp.maximum(
        jnp.maximum(in_ref[0, depth:], in_ref[1, depth:]), jnp.maximum(in_ref[2, depth:], in_ref[3, depth:])
    )
    for distant in range(far):
        base = FAR_ORDER.index(distant) * (rows + 1) + rows
        out_ref[base : base + 1, :] = tail[distant : distant + 1]


def near_sum(parts, far, rows):
    return pl.pallas_call(
        functools.partial(near_kernel, far=far, rows=rows),
        out_shape=pltpu.VMEM((far * (rows + 1), HALF), jnp.float32),
        name="near_sum",
    )(in_vmem(parts))


def far_kernel(in_ref, block_ref, peak_ref, *, far, rows):
    sums = [in_ref[k * (rows + 1) : k * (rows + 1) + rows, :] for k in range(far)]
    peaks = [in_ref[k * (rows + 1) + rows : (k + 1) * (rows + 1), :] for k in range(far)]
    block_ref[...] = jnp.broadcast_to(functools.reduce(jnp.add, sums), block_ref.shape)
    peak_ref[...] = jnp.broadcast_to(functools.reduce(jnp.maximum, peaks), peak_ref.shape)


def far_sum(parts, far, rows, copies):
    return pl.pallas_call(
        functools.partial(far_kernel, far=far, rows=rows),
        out_shape=(pltpu.VMEM((copies, rows, HALF), jnp.float32), pltpu.VMEM((8, HALF), jnp.float32)),
        name="far_sum",
    )(in_vmem(parts))


def parted(value):
    high = value.astype(jnp.bfloat16)
    return high, (value - high.astype(jnp.float32)).astype(jnp.bfloat16)


def single(left, right, dims=(((1,), (0,)), ((), ()))):
    return lax.dot_general(left, right, dims, preferred_element_type=jnp.float32)


def product(left, right):
    return single(left[0], right[0]) + (single(left[0], right[1]) + single(left[1], right[0]))


def final_kernel(all_ref, own_ref, peak_ref, weight_ref, out_ref, *, feats):
    count = all_ref.shape[0]
    whole = jnp.concatenate(
        [
            all_ref[:, :feats, :].reshape(count * feats, HALF),
            all_ref[:, feats:, :].reshape(count * feats, HALF),
        ],
        axis=1,
    )
    high, low = parted(whole)
    over_rows = (((0,), (0,)), ((), ()))
    mixed = single(high, low, over_rows)
    gram = single(high, high, over_rows) + (mixed + mixed.T)
    total = jnp.sum(whole * whole)
    factor = 1.0 / (jnp.sqrt(jnp.broadcast_to(total, (1, KD))) + 1e-07)
    row = lax.broadcasted_iota(jnp.int32, (KD, KD), 0)
    col = lax.broadcasted_iota(jnp.int32, (KD, KD), 1)
    first = gram * (factor * factor)
    split_first = parted(first)
    poly = jnp.where(row == col, coef_first, 0.0) + coef_second * first + coef_third * product(split_first, split_first)
    split_poly = parted(poly)
    own = jnp.concatenate([own_ref[0, :feats, :], own_ref[0, feats:, :]], axis=1) * factor
    current = product(parted(own), split_poly)
    second = parted(product(parted(product(split_poly, split_first)), split_poly))
    once = product(parted(current), second)
    twice = product(parted(once), second)
    ortho = coef_first * current + coef_second * once + coef_third * twice
    scale = 0.2 * math.sqrt(max(KR, KD))
    weight = weight_ref[...]
    stepped = weight - learn_rate * (scale * ortho + decay_rate * weight)
    root = jnp.sqrt(jnp.minimum(1.0, tau_logit / peak_ref[:1, :]))
    clip = jnp.concatenate([root, jnp.ones((1, KD - NOPE), jnp.float32)], axis=1)
    out_ref[...] = stepped * clip


def finish(blocks, own, peak, weight):
    return pl.pallas_call(
        functools.partial(final_kernel, feats=weight.shape[0]),
        out_shape=jax.ShapeDtypeStruct(weight.shape, jnp.float32),
        name="finish",
    )(in_vmem(blocks), in_vmem(own), in_vmem(peak), in_vmem(weight))


def stage_groups(size):
    chips = size // CORES
    near = []
    for core in range(CORES):
        for window in range(chips // NEAR):
            members = [(NEAR * window + core * (NEAR // 2) + k) % chips for k in range(NEAR)]
            near.append([CORES * z + core for z in sorted(members, key=lambda z: NEAR_ORDER.index(z % NEAR))])
    far = [
        [CORES * (kind + NEAR * k) + core for k in FAR_ORDER] for kind in range(NEAR) for core in range(CORES)
    ]
    return near, far


def body(kv_latent, kv_grad_out, kv_weight, logit_max, size, cols):
    far = size // (NEAR * CORES)
    feats = kv_latent.shape[1]
    rows = 2 * feats
    near, distant = stage_groups(size)

    def exchange(value, groups):
        return lax.all_to_all(value, "dp", 0, 0, axis_index_groups=groups, tiled=True)

    latent = kv_latent.T
    sent = partial_sums(latent, kv_grad_out, logit_max, far, True)
    taken = lax.ppermute(sent, "dp", [(i, i ^ 1) for i in range(size)])
    kept = partial_sums(latent, kv_grad_out, logit_max, far, False)
    is_sum = lax.broadcasted_iota(jnp.int32, kept.shape, 1) < far * rows
    parts = jnp.where(is_sum, kept + taken, jnp.maximum(kept, taken))
    summed = near_sum(exchange(parts, near), far, rows)
    parts = exchange(summed.reshape(far, 1, -1), distant).reshape(summed.shape)
    copies, peak = far_sum(parts, far, rows, cols)
    blocks = lax.all_to_all(copies, "cols", 0, 0, axis_index_groups=[list(COL_ORDER)], tiled=True)
    return finish(blocks, copies, peak, kv_weight)


def solution(mesh):
    in_specs = (P("dp", "cols"), P("dp", None), P("cols", "dp"), P("dp", None))
    out_specs = P("cols", "dp")
    size, cols = mesh.shape["dp"], mesh.shape["cols"]
    return jax.shard_map(
        lambda *args: body(*args, size, cols), mesh=mesh, in_specs=in_specs, out_specs=out_specs, check_vma=False
    )
```
